128 devices in a mesh: pts: 16 (over z_hi, x, core), mem: 8 (over z_lo, y).
Axes of the slice: x: 4, y: 4, z: 4 (z_hi: 2, z_lo: 2; z = z_hi * 2 + z_lo), core: 2. Of those that a mesh axis runs over, the one named last changes fastest.
Arguments:
- ensemble: bfloat16 [128, 128, 8192], P('mem', None, 'pts'), may hold values from -4 to 4
- increment: float32 [128, 8192], P(None, 'pts'), may hold values from -8 to 8
- obs_weight: float32 [128, 8192], P(None, 'pts'), may hold values from 0.3 to 3
- vertical: bfloat16 [128, 128], replicated, may hold values from -0.5 to 0.5
- block_table: bfloat16 [12, 128, 128], replicated, may hold values from -0.15625 to 0.15625
- block_cols: int32 [64, 12], replicated, may hold values from 0 to 63, as said below
Outputs:
- weighted: float32 [128, 8192], P(None, 'pts')
- applied: float32 [128, 8192], P(None, 'pts')
The draws below stay inside these ranges and needn't reach their ends.
Inputs may be any that keep to these rules, and one draw needn't show every extreme that they name: `block_cols`: row r begins with r itself, and its 12 entries are different block indices.
All inputs are finite; a program needn't handle non-finite values.
Results may differ from the reference program's by a relative error of at most 0.012.
Values may be sent and summed in bfloat16 or wider, within the bound.
A program may use at most 128 MiB of HBM per device.

```python
import math
import jax
import jax.numpy as jnp
from jax import lax

LV = 128
BLK = 128
NCOL = 12
P_SIZE = 8192
NB = 64
MEMBERS = 128


def draw_block_cols(key, part):
    row_keys = jax.random.split(jax.random.fold_in(key, 7), NB)
    orders = jax.vmap(lambda one_key: jax.random.permutation(one_key, NB - 1))(row_keys)[:, :NCOL - 1]
    row_ids = jnp.arange(NB, dtype=jnp.int32)[:, None]
    orders = orders.astype(jnp.int32)
    others = jnp.where(orders >= row_ids, orders + 1, orders)
    return jnp.concatenate([row_ids, others], axis=1).astype(jnp.int32)


def steps_of(stream_key, extent, cuts, low, high):
    factor_of, own = 1.0, jax.random.fold_in(stream_key, 6)
    for axis_at, parts in cuts:
        heights = jnp.exp(jax.random.uniform(jax.random.fold_in(own, axis_at), (parts,), jnp.float32, low / len(cuts), high / len(cuts)))
        factor_of = factor_of * jnp.repeat(heights, extent[axis_at] // parts).reshape([-1 if axis == axis_at else 1 for axis in range(len(extent))])
    return factor_of


def normal_values(key, dims, width, reach, cuts=(), kind=jnp.bfloat16):
    entries = jax.random.normal(key, dims, jnp.float32) * width
    if len(cuts) > 0:
        entries = steps_of(key, dims, cuts, -0.22, 0.18) * entries
    return jnp.clip(entries, min=-reach, max=reach).astype(kind)


def setup_inputs(seed: int = 0) -> dict:
    key_list = jax.random.split(jax.random.key(seed), 7)
    ensemble = normal_values(key_list[0], (MEMBERS, LV, P_SIZE), 0.3, 4.0, ((0, 8), (2, 16)))
    increment = normal_values(key_list[1], (LV, P_SIZE), 1.0, 8.0, ((1, 16),), jnp.float32)
    obs_weight = jnp.clip(jnp.exp(math.log(3.0) - 2.3025851 * jax.random.uniform(key_list[2], (LV, P_SIZE), jnp.float32) ** steps_of(key_list[2], (LV, P_SIZE), ((1, 16),), -0.2, 0.2)), 0.3, 3.0)
    vertical = normal_values(key_list[3], (LV, LV), LV ** -0.5, 0.5)
    block_table = normal_values(key_list[4], (NCOL, BLK, BLK), (NCOL * BLK) ** -0.5, 0.15625)
    block_cols = draw_block_cols(jax.random.fold_in(key_list[6], 71), 0)
    return dict(ensemble=ensemble, increment=increment, obs_weight=obs_weight, vertical=vertical, block_table=block_table, block_cols=block_cols)


def localize(values, block_table, block_cols):
    leading = values.shape[0]
    flattened = values.reshape(leading, NB, BLK)

    def add_slot(column, running):
        chosen = lax.dynamic_index_in_dim(block_cols, column, 1, keepdims=False)
        picked = jnp.take(flattened, chosen, axis=1).astype(jnp.float32)
        kernel = lax.dynamic_index_in_dim(block_table, column, 0, keepdims=False).astype(jnp.float32)
        return running + jnp.einsum("rnk,lk->rnl", picked, kernel)

    running = lax.fori_loop(0, NCOL, add_slot, jnp.zeros((leading, NB, BLK), jnp.float32))
    return running.reshape(leading, P_SIZE).astype(jnp.bfloat16)


def cov_apply(field_now, ensemble, vertical, block_table, block_cols):
    def member_step(summed, member):
        product = (member.astype(jnp.float32) * field_now).astype(jnp.bfloat16)
        vert_local = jnp.dot(vertical, product, preferred_element_type=jnp.float32).astype(jnp.bfloat16)
        horiz_local = lax.optimization_barrier(localize(vert_local, block_table, block_cols))
        return summed + member.astype(jnp.float32) * horiz_local.astype(jnp.float32), None

    summed, _ = lax.scan(member_step, jnp.zeros((LV, P_SIZE), jnp.float32), ensemble)
    return summed


def reference(ensemble, increment, obs_weight, vertical, block_table, block_cols):
    first_sum = cov_apply(increment, ensemble, vertical, block_table, block_cols)
    weighted = obs_weight * first_sum
    applied = cov_apply(weighted, ensemble, vertical, block_table, block_cols)
    return weighted, applied
```

```python
import jax
import jax.numpy as jnp
from jax import lax
from jax.experimental import pallas as pl
from jax.experimental.pallas import tpu as pltpu
from jax.sharding import PartitionSpec as P

MESH = pl.DeviceIdType.MESH
BF = jnp.bfloat16
F32 = jnp.float32

SPREAD = (
    (1, 1, 0), (0, 3, 0), (1, 3, 1), (0, 1, 1), (1, 0, 0), (0, 2, 0), (1, 2, 1), (0, 2, 1),
    (1, 2, 0), (1, 0, 1), (1, 3, 0), (0, 1, 0), (1, 1, 1), (0, 3, 1), (0, 0, 1),
)
PLANE = tuple((db, dz) for db in range(4) for dz in range(4) if (db, dz) != (0, 0))


def device(zhi, x, core, zlo, y):
    return ((zhi * 4 + x) * 2 + core, zlo * 4 + y)


def kernel(
    ens_hbm, inc_hbm, obs_hbm, vert_ref, table_ref, cols_ref,
    weighted_ref, applied_ref,
    ens, vl, tt, piece, obs,
    f1, f2, xo1, xo2, xi1, xi2, r1, r2, q1, q2, s1, s2, w1, w2, last,
    local_sem, es_sem, er_sem,
    gs1, gr1, gs2, gr2, gs3, gr3,
    cs, cr, as_, ar, bs, br, ls, lr,
):
    p, g = lax.axis_index("pts"), lax.axis_index("mem")
    zhi, x, core = p // 8, (p // 2) % 4, p % 2
    zlo, y = g // 4, g % 4
    zz = zhi * 2 + zlo
    partner = device(zhi, x, 1 - core, zlo, y)

    def pick(flat):
        return flat * y + (1 - flat) * x, flat * x + (1 - flat) * y

    def ring_peer(flat, a):
        return device(zhi, flat * x + (1 - flat) * a, core, zlo, flat * a + (1 - flat) * y)

    def plane_peer(flat, b, z):
        return device(z // 2, flat * b + (1 - flat) * x, core, z % 2, flat * y + (1 - flat) * b)

    def remote(src, dst, send, recv, to):
        return pltpu.make_async_remote_copy(
            src_ref=src, dst_ref=dst, send_sem=send, recv_sem=recv,
            device_id=to, device_id_type=MESH,
        )

    inc_copy = pltpu.make_async_copy(
        inc_hbm.at[pl.ds(pl.multiple_of(g * 16, 16), 16)], piece, local_sem.at[0])
    obs_copy = pltpu.make_async_copy(
        obs_hbm.at[pl.ds(pl.multiple_of(g * 16, 16), 16)], obs, local_sem.at[1])
    own_copy = pltpu.make_async_copy(ens_hbm.at[p], ens.at[p], local_sem.at[2])
    inc_copy.start()
    obs_copy.start()
    own_copy.start()

    spread_to = [
        device((zhi + dz) % 2, (x + dx) % 4, (core + dc) % 2, zlo, y) for dz, dx, dc in SPREAD
    ]
    by_core = 1 - core

    barrier = pltpu.get_barrier_semaphore()
    greet = list(spread_to)
    for flat in (1, by_core):
        a, b = pick(flat)
        greet += [ring_peer(flat, (a + d) % 4) for d in (1, 2, 3)]
        greet += [plane_peer(flat, (b + db) % 4, (zz + dz) % 4) for db, dz in PLANE]
    mem_peers = [(p, (g + d) % 8) for d in range(1, 8)]
    greet += mem_peers
    for to in greet:
        pl.semaphore_signal(barrier, inc=1, device_id=to, device_id_type=MESH)
    pl.semaphore_wait(barrier, len(greet))

    inc_copy.wait()

    def gather(n, f, flat, between):
        a, b = pick(flat)
        first = []
        for k, (db, dz) in enumerate(PLANE):
            mine = f.at[core, a, b, zz]
            copy = remote(mine, mine, gs1.at[n, k], gr1.at[n, b * 4 + zz],
                          plane_peer(flat, (b + db) % 4, (zz + dz) % 4))
            copy.start()
            first.append(copy)
        between()
        for db, dz in PLANE:
            bb, z2 = (b + db) % 4, (zz + dz) % 4
            slot = f.at[core, a, bb, z2]
            remote(slot, slot, gs1.at[n, 0], gr1.at[n, bb * 4 + z2], partner).wait_recv()
        second = []
        for d in (1, 2, 3):
            mine = f.at[core, a]
            copy = remote(mine, mine, gs2.at[n, d], gr2.at[n, a], ring_peer(flat, (a + d) % 4))
            copy.start()
            second.append(copy)
        third = []
        for d in range(4):
            aa = (a + d) % 4
            slot = f.at[core, aa]
            if d:
                remote(slot, slot, gs2.at[n, 0], gr2.at[n, aa], partner).wait_recv()
            copy = remote(slot, slot, gs3.at[n, d], gr3.at[n, aa], partner)
            copy.start()
            third.append(copy)
        return first + second + third

    def gather_rest(n, f):
        for a in range(4):
            slot = f.at[1 - core, a]
            remote(slot, slot, gs3.at[n, 0], gr3.at[n, a], partner).wait_recv()

    def field_at(f, flat, zhi2, x2, core2):
        rows = []
        for zl in range(2):
            for yy in range(4):
                rows.append(f[core2, flat * yy + (1 - flat) * x2, flat * x2 + (1 - flat) * yy, zhi2 * 2 + zl])
        return jnp.concatenate(rows, axis=0)

    def vertical_part(f, flat_of, core2, wait):
        flat = flat_of(core2)

        def one(i, carry):
            p2 = i * 2 + core2
            if wait:
                @pl.when(p2 != p)
                def _():
                    slot = ens.at[p2]
                    remote(slot, slot, es_sem.at[0], er_sem.at[p2], partner).wait_recv()
            field = field_at(f, flat, i // 4, i % 4, core2)
            product = (ens[p2].astype(F32) * field.astype(F32)).astype(BF)
            mixed = jnp.dot(vert_ref[...], product, preferred_element_type=F32).astype(BF)
            for k in range(4):
                vl[p2 * 4 + k] = mixed[:, k * 128:(k + 1) * 128]
            return carry

        lax.fori_loop(0, 8, one, 0)

    def horizontal(p2):
        parts = []
        for k in range(4):
            total = None
            for s in range(0, 12, 2):
                left = vl[cols_ref[(p2 * 4 + k) * 12 + s]]
                right = vl[cols_ref[(p2 * 4 + k) * 12 + s + 1]]
                term = jnp.dot(jnp.concatenate([left, right], axis=1),
                               tt[s * 128:(s + 2) * 128], preferred_element_type=F32)
                total = term if total is None else total + term
            parts.append(total.astype(BF))
        local = jnp.concatenate(parts, axis=1)
        return ens[p2].astype(F32) * local.astype(F32)

    def scatter(n, xo, xi, r, q, s_buf, w):
        flat = by_core
        a, b = pick(flat)

        def away(i, carry):
            x2, zh = i // 2, i % 2
            p2 = (zh * 4 + x2) * 2 + 1 - core
            xo[i] = horizontal(p2).astype(BF)
            remote(xo.at[i], xi.at[i], cs.at[n, i], cr.at[n, i], partner).start()
            return carry

        lax.fori_loop(0, 8, away, 0)

        def ring_copy(x2, yy):
            a2, b2 = flat * yy + (1 - flat) * x2, flat * x2 + (1 - flat) * yy
            return a2, remote(r.at[a2, b2], q.at[a, b2], as_.at[n, a2 * 4 + b2],
                              ar.at[n, a * 4 + b2], ring_peer(flat, a2))

        def keep(x2, carry):
            for zh in range(2):
                i = x2 * 2 + zh
                p2 = (zh * 4 + x2) * 2 + core
                mine = horizontal(p2)
                remote(xo.at[i], xi.at[i], cs.at[n, i], cr.at[n, i], partner).wait_recv()
                both = (mine + xi[i].astype(F32)).astype(BF)
                for zl in range(2):
                    for yy in range(4):
                        a2, b2 = flat * yy + (1 - flat) * x2, flat * x2 + (1 - flat) * yy
                        r[a2, b2, zh * 2 + zl] = both[zl * 64 + yy * 16:zl * 64 + yy * 16 + 16]
            for yy in range(4):
                a2, copy = ring_copy(x2, yy)

                @pl.when(a2 != a)
                def _():
                    copy.start()
            return carry

        lax.fori_loop(0, 4, keep, 0)

        def plane_copy(b2, z2):
            return remote(s_buf.at[b2, z2], w.at[b * 4 + zz], bs.at[n, b2 * 4 + z2],
                          br.at[n, b * 4 + zz], plane_peer(flat, b2, z2))

        for b2 in range(4):
            for d in (1, 2, 3):
                aa = (a + d) % 4
                slot = q.at[aa, b2]
                remote(slot, slot, as_.at[n, 0], ar.at[n, aa * 4 + b2], partner).wait_recv()
            total = r[a, b2].astype(F32)
            for d in (1, 2, 3):
                total = total + q[(a + d) % 4, b2].astype(F32)
            s_buf[b2] = total.astype(BF)
            for z2 in range(4):
                @pl.when(jnp.logical_or(b != b2, zz != z2))
                def _():
                    plane_copy(b2, z2).start()
        total = s_buf[b, zz].astype(F32)
        for db, dz in PLANE:
            k = (b + db) % 4 * 4 + (zz + dz) % 4
            remote(w.at[k], w.at[k], bs.at[n, 0], br.at[n, k], partner).wait_recv()
            total = total + w[k].astype(F32)

        def finish():
            for i in range(8):
                remote(xo.at[i], xi.at[i], cs.at[n, i], cr.at[n, i], partner).wait_send()
            for x2 in range(4):
                for yy in range(4):
                    a2, copy = ring_copy(x2, yy)

                    @pl.when(a2 != a)
                    def _():
                        copy.wait_send()
            for b2 in range(4):
                for z2 in range(4):
                    @pl.when(jnp.logical_or(b != b2, zz != z2))
                    def _():
                        plane_copy(b2, z2).wait_send()

        return total, finish

    a1, b1 = pick(1)
    f1[core, a1, b1, zz] = piece[...].astype(BF)
    spread = []

    def start_spread():
        for k, (dz, dx, dc) in enumerate(SPREAD):
            to = spread_to[k]
            copy = remote(ens_hbm.at[to[0]], ens.at[p], es_sem.at[k], er_sem.at[p], to)
            copy.start()
            spread.append(copy)
        for s in range(12):
            tt[s * 128:(s + 1) * 128] = table_ref[s].T

    sent = gather(0, f1, 1, start_spread)
    own_copy.wait()
    vertical_part(f1, lambda c: 1, core, True)
    gather_rest(0, f1)
    vertical_part(f1, lambda c: 1, 1 - core, True)
    first, finish1 = scatter(0, xo1, xi1, r1, q1, s1, w1)

    obs_copy.wait()
    a2, b2 = pick(by_core)
    f2[core, a2, b2, zz] = (first * obs[...]).astype(BF)
    sent += gather(1, f2, by_core, lambda: None)
    vertical_part(f2, lambda c: 1 - c, core, False)
    weighted_ref[...] = field_at(f2, by_core, zhi, x, core).astype(F32)
    gather_rest(1, f2)
    vertical_part(f2, lambda c: 1 - c, 1 - core, False)
    second, finish2 = scatter(1, xo2, xi2, r2, q2, s2, w2)

    last[g] = second
    out = []
    for k, to in enumerate(mem_peers):
        copy = remote(last.at[g], last.at[g], ls.at[k], lr.at[g], to)
        copy.start()
        out.append(copy)
    finish1()
    finish2()
    for copy in spread + sent:
        copy.wait_send()
    for d in range(1, 8):
        k = (g + d) % 8
        remote(last.at[k], last.at[k], ls.at[0], lr.at[k], partner).wait_recv()
    for k in range(8):
        applied_ref[k * 16:(k + 1) * 16] = last[k]
    for copy in out:
        copy.wait_send()


def per_device(ensemble, increment, obs_weight, vertical, block_table, block_cols):
    dma = pltpu.SemaphoreType.DMA
    vmem = pl.BlockSpec(memory_space=pltpu.VMEM)
    hbm = pl.BlockSpec(memory_space=pl.ANY)
    field = pltpu.VMEM((2, 4, 4, 4, 16, 512), BF)
    return pl.pallas_call(
        kernel,
        out_shape=(jax.ShapeDtypeStruct((128, 512), F32), jax.ShapeDtypeStruct((128, 512), F32)),
        in_specs=[hbm, hbm, hbm, vmem, vmem, pl.BlockSpec(memory_space=pltpu.SMEM)],
        out_specs=(vmem, vmem),
        scratch_shapes=[
            pltpu.VMEM((16, 128, 512), BF),
            pltpu.VMEM((64, 128, 128), BF),
            pltpu.VMEM((12 * 128, 128), BF),
            pltpu.VMEM((16, 512), F32),
            pltpu.VMEM((16, 512), F32),
            field, field,
        ] + [pltpu.VMEM((8, 128, 512), BF)] * 4
        + [pltpu.VMEM((4, 4, 4, 16, 512), BF)] * 4
        + [pltpu.VMEM((4, 4, 16, 512), BF)] * 2
        + [pltpu.VMEM((16, 16, 512), BF)] * 2
        + [
            pltpu.VMEM((8, 16, 512), F32),
            dma((3,)), dma((15,)), dma((16,)),
            dma((2, 15)), dma((2, 16)), dma((2, 4)), dma((2, 4)), dma((2, 4)), dma((2, 4)),
            dma((2, 8)), dma((2, 8)), dma((2, 16)), dma((2, 16)), dma((2, 16)), dma((2, 16)),
            dma((7,)), dma((8,)),
        ],
        compiler_params=pltpu.CompilerParams(
            collective_id=0, has_side_effects=True, vmem_limit_bytes=48 * 1024 * 1024),
        name="covariance",
    )(ensemble, increment, obs_weight, vertical, block_table, block_cols.reshape(-1))


def solution(mesh):
    return jax.shard_map(
        per_device,
        mesh=mesh,
        in_specs=(P("mem", None, "pts"), P(None, "pts"), P(None, "pts"), P(), P(), P()),
        out_specs=(P(None, "pts"), P(None, "pts")),
        check_vma=False,
    )
```

```python
import jax
import jax.numpy as jnp
from jax import lax
from jax.experimental import pallas as pl
from jax.experimental.pallas import tpu as pltpu
from jax.sharding import PartitionSpec as P

MESH = pl.DeviceIdType.MESH
BF = jnp.bfloat16
F32 = jnp.float32

SPREAD = (
    (0, 3, 0), (0, 1, 0), (1, 1, 1), (0, 3, 1), (1, 2, 1), (1, 3, 0), (1, 0, 0), (1, 0, 1),
    (0, 2, 1), (1, 2, 0), (1, 3, 1), (0, 1, 1), (0, 2, 0), (1, 1, 0), (0, 0, 1),
)
ORDER = (2, 1, 3, 0)
BACK = (2, 3, 1, 0)


def device(zhi, x, core, zlo, y):
    return ((zhi * 4 + x) * 2 + core, zlo * 4 + y)


def remote(src, dst, send, recv, to):
    return pltpu.make_async_remote_copy(
        src_ref=src, dst_ref=dst, send_sem=send, recv_sem=recv, device_id=to, device_id_type=MESH)


def kernel(
    ens_hbm, inc_hbm, obs_hbm, vert_hbm, table_hbm, cols_ref,
    out_ref,
    arrived, ens, vl, tcat, vert, inc, obs,
    f1, f2, xo1, xo2, xi1, xi2, r1, r2, q1, q2, s1, s2, w1, w2, last,
    local_sem, es_sem, er_sem,
    gs1, gr1, gs2, gr2, gs3, gr3, hs1, hr1, hs2, hr2, hs3, hr3,
    cs, cr, as_, ar, bs, br, ls, lr,
):
    p, g = lax.axis_index("pts"), lax.axis_index("mem")
    zhi, x, core = p // 8, (p // 2) % 4, p % 2
    zlo, y = g // 4, g % 4
    zz = zhi * 2 + zlo
    other = 1 - core
    partner = device(zhi, x, other, zlo, y)
    flat = other
    a, b = flat * y + core * x, flat * x + core * y
    half = pl.ds(pl.multiple_of(zlo * 64, 64), 64)

    def ring_peer(a2):
        return device(zhi, flat * x + core * a2, core, zlo, flat * a2 + core * y)

    def plane_peer(b2, z2):
        return device(z2 // 2, flat * b2 + core * x, core, z2 % 2, flat * y + core * b2)

    def landed(ref, sem):
        remote(ref, ref, es_sem.at[0], sem, partner).wait_recv()

    def block_of(core2, a2, b2, zh):
        return ((zh * 4 + (1 - core2) * b2 + core2 * a2) * 2 + core2) * 4 + (1 - core2) * a2 + core2 * b2

    mine = pl.ds(pl.multiple_of(y * 128, 128), 128)
    local = [
        pltpu.make_async_copy(inc_hbm.at[:, mine], inc, local_sem.at[0]),
        pltpu.make_async_copy(obs_hbm.at[:, mine], obs, local_sem.at[1]),
        pltpu.make_async_copy(ens_hbm.at[p], arrived.at[p], local_sem.at[2]),
        pltpu.make_async_copy(vert_hbm, vert, local_sem.at[3]),
    ]
    for s in range(12):
        local.append(pltpu.make_async_copy(
            table_hbm.at[s], tcat.at[:, pl.ds(s * 128, 128)], local_sem.at[4 + s]))
    for copy in local:
        copy.start()

    spread_to = [
        device((zhi + dz) % 2, (x + dx) % 4, (core + dc) % 2, zlo, y) for dz, dx, dc in SPREAD
    ]
    mem_peers = [(p, (g + d) % 8) for d in range(1, 8)]
    far = [
        device(flat * ((zhi + k // 4) % 2) + core * (1 - zhi), flat * ((x + k % 4) % 4) + core * x, core,
               flat * (1 - zlo) + core * ((zlo + k // 4) % 2), flat * y + core * ((y + k % 4) % 4))
        for k in range(1, 8)
    ]
    barrier = pltpu.get_barrier_semaphore()
    greet = spread_to + mem_peers + far
    for to in greet:
        pl.semaphore_signal(barrier, inc=1, device_id=to, device_id_type=MESH)

    sent = []
    local[0].wait()
    f1[core, y, x, zhi] = inc[...].T.astype(BF)

    def share(k):
        own = f1.at[core, y, x, zhi]
        copy = remote(own, own, gs1.at[k], gr1.at[zhi * 4 + x],
                      device((zhi + k // 4) % 2, (x + k % 4) % 4, core, zlo, y))
        copy.start()
        sent.append(copy)

    def spread(k):
        to = spread_to[k]
        copy = remote(ens_hbm.at[to[0]], arrived.at[p], es_sem.at[k], er_sem.at[p], to)
        copy.start()
        sent.append(copy)

    pl.semaphore_wait(barrier, len(greet))
    for k in (1, 3, 4, 2, 5, 7, 6):
        share(k)
    for k in range(15):
        spread(k)
    for k in range(1, 8):
        x2, zh = (x + k % 4) % 4, (zhi + k // 4) % 2
        landed(f1.at[core, y, x2, zh], gr1.at[zh * 4 + x2])
    own = f1.at[core, y]
    for d in (1, 2, 3):
        copy = remote(own, own, gs2.at[d], gr2.at[y], device(zhi, x, core, zlo, (y + d) % 4))
        copy.start()
        sent.append(copy)
    for d in range(4):
        slot = f1.at[core, (y + d) % 4]
        if d:
            landed(slot, gr2.at[(y + d) % 4])
        copy = remote(slot, slot, gs3.at[d], gr3.at[(y + d) % 4], partner)
        copy.start()
        sent.append(copy)
    for d in range(4):
        landed(f1.at[other, (y + d) % 4], gr3.at[(y + d) % 4])

    def mix(product):
        return lax.dot_general(product.astype(BF), vert[...], (((1,), (1,)), ((), ())),
                               preferred_element_type=F32).astype(BF)

    local[3].wait()
    for k in range(16):
        dz, dx, dc = (0, 0, 0) if k == 0 else SPREAD[k - 1]
        zh, x2, core2 = (zhi + dz) % 2, (x + 4 - dx) % 4, (core + dc) % 2
        p2 = (zh * 4 + x2) * 2 + core2
        if k == 0:
            local[2].wait()
        else:
            landed(arrived.at[p2], er_sem.at[p2])
        products = []
        for yy in range(4):
            share = arrived[p2, :, yy * 128:(yy + 1) * 128].T
            ens[p2 * 4 + yy] = share
            products.append((share.astype(F32) * f1[core2, yy, x2, zh].astype(F32)).astype(BF))
        mixed = mix(jnp.concatenate(products, axis=0))
        for yy in range(4):
            vl[p2 * 4 + yy] = mixed[yy * 128:(yy + 1) * 128]
    for s in range(12):
        local[4 + s].wait()

    def vertical(f, core2, a2):
        products = []
        blocks = []
        for b2 in range(4):
            for zh in range(2):
                r = block_of(core2, a2, b2, zh)
                blocks.append(r)
                products.append((ens[r].astype(F32) * f[core2, a2, b2, zh].astype(F32)).astype(BF))
        mixed = mix(jnp.concatenate(products, axis=0))
        for k, r in enumerate(blocks):
            vl[r] = mixed[k * 128:(k + 1) * 128]

    def horizontal(core2, a2):
        blocks = [block_of(core2, a2, b2, zh) for b2 in range(4) for zh in range(2)]
        stacked = jnp.concatenate(
            [jnp.concatenate([vl[cols_ref[s, r]] for s in range(12)], axis=0) for r in blocks], axis=1)
        total = jnp.dot(tcat[...], stacked, preferred_element_type=F32).astype(BF)
        return [ens[r].astype(F32) * total[:, k * 128:(k + 1) * 128].astype(F32)
                for k, r in enumerate(blocks)]

    def step_of(t):
        return jnp.where(t == 0, 2, jnp.where(t == 1, 1, jnp.where(t == 2, 3, 0)))

    def scatter(n, xo, xi, r, q, s_buf, w):
        a_other = flat * x + core * y

        def core_copy(t):
            return remote(xo.at[t], xi.at[t], cs.at[n, t], cr.at[n, t], partner)

        def away(t):
            for k, value in enumerate(horizontal(other, (a_other + step_of(t)) % 4)):
                xo[t, k] = value.astype(BF)
            core_copy(t).start()

        def keep(t):
            values = horizontal(core, (a + step_of(t)) % 4)
            core_copy(t).wait_recv()
            for k, value in enumerate(values):
                r[t, k // 2, k % 2] = (value + xi[t, k].astype(F32)).astype(BF)

        def ring_copy(t, b2):
            return remote(r.at[t, b2], q.at[t, b2], as_.at[n, t, b2], ar.at[n, t, b2],
                          ring_peer((a + step_of(t)) % 4))

        def both(t, carry):
            away(t + 1)
            keep(t)
            for d in ORDER:
                ring_copy(t, (b + d) % 4).start()
            return carry

        away(0)
        lax.fori_loop(0, 3, both, 0)
        keep(3)

        def plane_copy(b2, z2):
            rows = pl.ds(pl.multiple_of((z2 % 2) * 64, 64), 64)
            return remote(s_buf.at[b2, z2 // 2, rows], w.at[b * 4 + zz], bs.at[n, b2 * 4 + z2],
                          br.at[n, b * 4 + zz], plane_peer(b2, z2))

        plane = []
        for d in ORDER:
            b2 = (b + d) % 4
            total = r[3, b2].astype(F32)
            for t in range(3):
                landed(q.at[t, b2], ar.at[n, t, b2])
                total = total + q[t, b2].astype(F32)
            s_buf[b2] = total.astype(BF)
            for dz in ORDER:
                if d or dz:
                    copy = plane_copy(b2, (zz + dz) % 4)
                    copy.start()
                    plane.append(copy)
        total = s_buf[b, zhi, half].astype(F32)
        for d in BACK:
            for dz in BACK:
                if d or dz:
                    k = (b + d) % 4 * 4 + (zz + dz) % 4
                    landed(w.at[k], br.at[n, k])
                    total = total + w[k].astype(F32)

        def finish():
            for t in range(4):
                core_copy(t).wait_send()
            for t in range(3):
                for b2 in range(4):
                    ring_copy(t, b2).wait_send()
            for copy in plane:
                copy.wait_send()

        return total, finish

    first, finish1 = scatter(0, xo1, xi1, r1, q1, s1, w1)

    local[1].wait()
    obs[...] = obs[...].T
    f2[core, a, b, zhi, half] = (first * obs[half]).astype(BF)

    def piece(a2, d, dz):
        b2, z2 = (b + d) % 4, (zz + dz) % 4
        rows = pl.ds(pl.multiple_of((z2 % 2) * 64, 64), 64)
        return f2.at[core, a2, b2, z2 // 2, rows], b2 * 4 + z2

    def pass_on(d, dz):
        slot, k = piece(a, d, dz)
        for da in (2, 1, 3):
            copy = remote(slot, slot, hs2.at[da, k], hr2.at[a, k], ring_peer((a + da) % 4))
            copy.start()
            sent.append(copy)

    pass_on(0, 0)
    own, k = piece(a, 0, 0)
    for d in (0, 1, 3, 2):
        for dz in (2, 1, 3, 0):
            if d or dz:
                copy = remote(own, own, hs1.at[d * 4 + dz], hr1.at[k],
                              plane_peer((b + d) % 4, (zz + dz) % 4))
                copy.start()
                sent.append(copy)
    for d in (0, 3, 1, 2):
        for dz in BACK:
            if d or dz:
                slot, k = piece(a, d, dz)
                landed(slot, hr1.at[k])
                pass_on(d, dz)
    def hand_over(a2, d):
        slot = f2.at[core, a2, (b + d) % 4]
        copy = remote(slot, slot, hs3.at[a2, d], hr3.at[a2, (b + d) % 4], partner)
        copy.start()
        sent.append(copy)

    a_other, b_other = flat * x + core * y, flat * y + core * x
    for d in (0, 3, 1, 2):
        hand_over(a, d)
    vertical(f2, core, a)
    for da in (0, 1, 3, 2):
        a2 = (a + da) % 4
        if da:
            for d in (0, 3, 1, 2):
                for dz in BACK:
                    slot, k = piece(a2, d, dz)
                    landed(slot, hr2.at[a2, k])
                hand_over(a2, d)
            vertical(f2, core, a2)
        a2 = (a_other + da) % 4
        for d in (0, 3, 1, 2):
            b2 = (b_other + d) % 4
            landed(f2.at[other, a2, b2], hr3.at[a2, b2])
        vertical(f2, other, a2)
    second, finish2 = scatter(1, xo2, xi2, r2, q2, s2, w2)

    last[g] = second.astype(BF)
    out = []
    for k, to in enumerate(mem_peers):
        copy = remote(last.at[g], last.at[g], ls.at[k], lr.at[g], to)
        copy.start()
        out.append(copy)
    for yy in range(4):
        block = f2[core, flat * yy + core * x, flat * x + core * yy, zhi]
        out_ref[0, :, yy * 128:(yy + 1) * 128] = block.T
    finish1()
    finish2()
    for copy in sent:
        copy.wait_send()
    for d in range(1, 8):
        k = (g + d) % 8
        landed(last.at[k], lr.at[k])
    for yy in range(4):
        block = jnp.concatenate([last[yy], last[4 + yy]], axis=0)
        out_ref[1, :, yy * 128:(yy + 1) * 128] = block.T
    for copy in out:
        copy.wait_send()


def per_device(ensemble, increment, obs_weight, vertical, block_table, block_cols):
    dma = pltpu.SemaphoreType.DMA
    vmem = pl.BlockSpec(memory_space=pltpu.VMEM)
    hbm = pl.BlockSpec(memory_space=pltpu.HBM)
    twice = lambda shape, kind=BF: [pltpu.VMEM(shape, kind)] * 2
    both = pl.pallas_call(
        kernel,
        out_shape=jax.ShapeDtypeStruct((2, 128, 512), BF),
        in_specs=[hbm, hbm, hbm, hbm, hbm, pl.BlockSpec(memory_space=pltpu.SMEM)],
        out_specs=vmem,
        scratch_shapes=[
            pltpu.VMEM((16, 128, 512), BF),
            pltpu.VMEM((64, 128, 128), BF),
            pltpu.VMEM((64, 128, 128), BF),
            pltpu.VMEM((128, 12 * 128), BF),
            pltpu.VMEM((128, 128), BF),
            pltpu.VMEM((128, 128), F32),
            pltpu.VMEM((128, 128), F32),
        ] + twice((2, 4, 4, 2, 128, 128)) + twice((4, 8, 128, 128)) + twice((4, 8, 128, 128))
        + twice((4, 4, 2, 128, 128)) + twice((3, 4, 2, 128, 128)) + twice((4, 2, 128, 128))
        + twice((16, 64, 128))
        + [
            pltpu.VMEM((8, 64, 128), BF),
            dma((16,)), dma((15,)), dma((16,)),
            dma((8,)), dma((8,)), dma((4,)), dma((4,)), dma((4,)), dma((4,)),
            dma((16,)), dma((16,)), dma((4, 16)), dma((4, 16)), dma((4, 4)), dma((4, 4)),
            dma((2, 4)), dma((2, 4)), dma((2, 3, 4)), dma((2, 3, 4)), dma((2, 16)), dma((2, 16)),
            dma((7,)), dma((8,)),
        ],
        compiler_params=pltpu.CompilerParams(
            collective_id=0, has_side_effects=True, vmem_limit_bytes=62 * 1024 * 1024),
        name="covariance",
    )(ensemble, increment, obs_weight, vertical, block_table, block_cols.T)
    return both[0].astype(F32), both[1].astype(F32)


def solution(mesh):
    return jax.shard_map(
        per_device,
        mesh=mesh,
        in_specs=(P("mem", None, "pts"), P(None, "pts"), P(None, "pts"), P(), P(), P()),
        out_specs=(P(None, "pts"), P(None, "pts")),
        check_vma=False,
    )
```

```python
import jax
import jax.numpy as jnp
from jax import lax
from jax.experimental import pallas as pl
from jax.experimental.pallas import tpu as pltpu
from jax.sharding import PartitionSpec as P

MESH = pl.DeviceIdType.MESH
BF = jnp.bfloat16
F32 = jnp.float32

SPREAD = (
    (0, 3, 0), (0, 1, 0), (1, 1, 1), (0, 3, 1), (1, 2, 1), (1, 3, 0), (1, 0, 0), (1, 0, 1),
    (0, 2, 1), (1, 2, 0), (1, 3, 1), (0, 1, 1), (0, 2, 0), (1, 1, 0), (0, 0, 1),
)
ORDER = (2, 1, 3, 0)
BACK = (2, 3, 1, 0)


def device(zhi, x, core, zlo, y):
    return ((zhi * 4 + x) * 2 + core, zlo * 4 + y)


def remote(src, dst, send, recv, to):
    return pltpu.make_async_remote_copy(
        src_ref=src, dst_ref=dst, send_sem=send, recv_sem=recv, device_id=to, device_id_type=MESH)


def kernel(
    ens_hbm, inc_hbm, obs_hbm, vert_hbm, table_hbm, cols_hbm,
    out_ref,
    cols_ref, arrived, ens, vl, tcat, vert, inc, obs,
    f1, f2, xo1, xo2, xi1, xi2, r1, r2, q1, q2, s1, s2, w1, w2, last,
    local_sem, es_sem, er_sem,
    gs1, gr1, gs2, gr2, gs3, gr3, hs1, hr1, hs2, hr2, hs3, hr3,
    cs, cr, as_, ar, bs, br, ls, lr,
):
    p, g = lax.axis_index("pts"), lax.axis_index("mem")
    zhi, x, core = p // 8, (p // 2) % 4, p % 2
    zlo, y = g // 4, g % 4
    zz = zhi * 2 + zlo
    other = 1 - core
    partner = device(zhi, x, other, zlo, y)
    flat = other
    a, b = flat * y + core * x, flat * x + core * y
    half = pl.ds(pl.multiple_of(zlo * 64, 64), 64)

    def ring_peer(a2):
        return device(zhi, flat * x + core * a2, core, zlo, flat * a2 + core * y)

    def plane_peer(b2, z2):
        return device(z2 // 2, flat * b2 + core * x, core, z2 % 2, flat * y + core * b2)

    def landed(ref, sem):
        remote(ref, ref, es_sem, sem, partner).wait_recv()

    def drained(ref, sem):
        remote(ref, ref, sem, er_sem.at[0], partner).wait_send()

    def blocks(n):
        return ens.at[pl.ds(0, n)]

    def pieces(n):
        return w1.at[pl.ds(0, n)]

    def block_of(core2, a2, b2, zh):
        return ((zh * 4 + (1 - core2) * b2 + core2 * a2) * 2 + core2) * 4 + (1 - core2) * a2 + core2 * b2

    mine = pl.ds(pl.multiple_of(y * 128, 128), 128)
    local = [
        pltpu.make_async_copy(inc_hbm.at[:, mine], inc, local_sem.at[0]),
        pltpu.make_async_copy(obs_hbm.at[:, mine], obs, local_sem.at[1]),
        pltpu.make_async_copy(ens_hbm.at[p], arrived.at[p], local_sem.at[2]),
        pltpu.make_async_copy(vert_hbm, vert, local_sem.at[3]),
    ]
    for s in range(12):
        local.append(pltpu.make_async_copy(
            table_hbm.at[s], tcat.at[:, pl.ds(s * 128, 128)], local_sem.at[4]))
    local.append(pltpu.make_async_copy(cols_hbm, cols_ref, local_sem.at[5]))
    for copy in local:
        copy.start()

    spread_to = [
        device((zhi + dz) % 2, (x + dx) % 4, (core + dc) % 2, zlo, y) for dz, dx, dc in SPREAD
    ]
    mem_peers = [(p, (g + d) % 8) for d in range(1, 8)]
    far = [
        device(flat * ((zhi + k // 4) % 2) + core * (1 - zhi), flat * ((x + k % 4) % 4) + core * x, core,
               flat * (1 - zlo) + core * ((zlo + k // 4) % 2), flat * y + core * ((y + k % 4) % 4))
        for k in range(1, 8)
    ]
    barrier = pltpu.get_barrier_semaphore()
    greet = spread_to + mem_peers + far
    for to in greet:
        pl.semaphore_signal(barrier, inc=1, device_id=to, device_id_type=MESH)

    local[0].wait()
    f1[core, y, x, zhi] = inc[...].T.astype(BF)

    def share(k):
        own = f1.at[core, y, x, zhi]
        copy = remote(own, own, gs1, gr1,
                      device((zhi + k // 4) % 2, (x + k % 4) % 4, core, zlo, y))
        copy.start()

    def spread(k):
        to = spread_to[k]
        copy = remote(ens_hbm.at[to[0]], arrived.at[p], es_sem, er_sem.at[p], to)
        copy.start()

    pl.semaphore_wait(barrier, len(greet))
    for k in (1, 3, 4, 2, 5, 7, 6):
        share(k)
    for k in range(15):
        spread(k)
    landed(blocks(7), gr1)
    own = f1.at[core, y]
    for d in (1, 2, 3):
        remote(own, own, gs2, gr2, device(zhi, x, core, zlo, (y + d) % 4)).start()
    landed(blocks(24), gr2)
    own = f1.at[core]
    remote(own, own, gs3, gr3, partner).start()
    landed(blocks(32), gr3)

    def mix(product):
        return lax.dot_general(product.astype(BF), vert[...], (((1,), (1,)), ((), ())),
                               preferred_element_type=F32).astype(BF)

    local[3].wait()
    for k in range(16):
        dz, dx, dc = (0, 0, 0) if k == 0 else SPREAD[k - 1]
        zh, x2, core2 = (zhi + dz) % 2, (x + 4 - dx) % 4, (core + dc) % 2
        p2 = (zh * 4 + x2) * 2 + core2
        if k == 0:
            local[2].wait()
        else:
            landed(arrived.at[p2], er_sem.at[p2])
        products = []
        for yy in range(4):
            share = arrived[p2, :, yy * 128:(yy + 1) * 128].T
            ens[p2 * 4 + yy] = share
            products.append((share.astype(F32) * f1[core2, yy, x2, zh].astype(F32)).astype(BF))
        mixed = mix(jnp.concatenate(products, axis=0))
        for yy in range(4):
            vl[p2 * 4 + yy] = mixed[yy * 128:(yy + 1) * 128]
    pltpu.make_async_copy(tcat, tcat, local_sem.at[4]).wait()
    local[-1].wait()

    def vertical(f, core2, a2):
        products = []
        blocks = []
        for b2 in range(4):
            for zh in range(2):
                r = block_of(core2, a2, b2, zh)
                blocks.append(r)
                products.append((ens[r].astype(F32) * f[core2, a2, b2, zh].astype(F32)).astype(BF))
        mixed = mix(jnp.concatenate(products, axis=0))
        for k, r in enumerate(blocks):
            vl[r] = mixed[k * 128:(k + 1) * 128]

    def horizontal(core2, a2):
        blocks = [block_of(core2, a2, b2, zh) for b2 in range(4) for zh in range(2)]
        stacked = jnp.concatenate(
            [jnp.concatenate([vl[cols_ref[s, r]] for s in range(12)], axis=0) for r in blocks], axis=1)
        total = jnp.dot(tcat[...], stacked, preferred_element_type=F32).astype(BF)
        return [ens[r].astype(F32) * total[:, k * 128:(k + 1) * 128].astype(F32)
                for k, r in enumerate(blocks)]

    def step_of(t):
        return jnp.where(t == 0, 2, jnp.where(t == 1, 1, jnp.where(t == 2, 3, 0)))

    def scatter(n, xo, xi, r, q, s_buf, w):
        a_other = flat * x + core * y

        def core_copy(t):
            return remote(xo.at[t], xi.at[t], cs.at[n], cr.at[n, t], partner)

        def away(t):
            for k, value in enumerate(horizontal(other, (a_other + step_of(t)) % 4)):
                xo[t, k] = value.astype(BF)
            core_copy(t).start()

        def keep(t):
            values = horizontal(core, (a + step_of(t)) % 4)
            core_copy(t).wait_recv()
            for k, value in enumerate(values):
                r[t, k // 2, k % 2] = (value + xi[t, k].astype(F32)).astype(BF)

        def ring_copy(t, b2):
            return remote(r.at[t, b2], q.at[t, b2], as_.at[n], ar.at[n, b2],
                          ring_peer((a + step_of(t)) % 4))

        def both(t, carry):
            away(t + 1)
            keep(t)
            for d in ORDER:
                ring_copy(t, (b + d) % 4).start()
            return carry

        away(0)
        lax.fori_loop(0, 3, both, 0)
        keep(3)

        def plane_copy(b2, z2):
            rows = pl.ds(pl.multiple_of((z2 % 2) * 64, 64), 64)
            return remote(s_buf.at[b2, z2 // 2, rows], w.at[b * 4 + zz], bs.at[n],
                          br.at[n], plane_peer(b2, z2))

        for d in ORDER:
            b2 = (b + d) % 4
            total = r[3, b2].astype(F32)
            landed(blocks(6), ar.at[n, b2])
            for t in range(3):
                total = total + q[t, b2].astype(F32)
            s_buf[b2] = total.astype(BF)
            for dz in ORDER:
                if d or dz:
                    plane_copy(b2, (zz + dz) % 4).start()
        total = s_buf[b, zhi, half].astype(F32)
        landed(pieces(15), br.at[n])
        for d in BACK:
            for dz in BACK:
                if d or dz:
                    k = (b + d) % 4 * 4 + (zz + dz) % 4
                    total = total + w[k].astype(F32)

        return total

    first = scatter(0, xo1, xi1, r1, q1, s1, w1)

    local[1].wait()
    obs[...] = obs[...].T
    f2[core, a, b, zhi, half] = (first * obs[half]).astype(BF)

    own = f2.at[core, a, b, zhi, half]
    for d in (0, 1, 3, 2):
        for dz in (2, 1, 3, 0):
            if d or dz:
                remote(own, own, hs1, hr1.at[b], plane_peer((b + d) % 4, (zz + dz) % 4)).start()
    for d in (0, 3, 1, 2):
        b2 = (b + d) % 4
        landed(pieces(4 if d else 3), hr1.at[b2])
        slot = f2.at[core, a, b2]
        for da in (2, 1, 3):
            remote(slot, slot, hs2, hr2.at[a, b2], ring_peer((a + da) % 4)).start()

    def hand_over(a2):
        slot = f2.at[core, a2]
        remote(slot, slot, hs3, hr3.at[a2], partner).start()

    hand_over(a)
    vertical(f2, core, a)
    for da in (0, 1, 3, 2):
        a2 = (a + da) % 4
        if da:
            for d in (0, 3, 1, 2):
                landed(blocks(2), hr2.at[a2, (b + d) % 4])
            hand_over(a2)
            vertical(f2, core, a2)
        a2 = (flat * x + core * y + da) % 4
        landed(blocks(8), hr3.at[a2])
        vertical(f2, other, a2)
    second = scatter(1, xo2, xi2, r2, q2, s2, w2)

    last[g] = second.astype(BF)
    for to in mem_peers:
        remote(last.at[g], last.at[g], ls, lr, to).start()
    for yy in range(4):
        block = f2[core, flat * yy + core * x, flat * x + core * yy, zhi]
        out_ref[0, :, yy * 128:(yy + 1) * 128] = block.T
    drained(arrived.at[pl.ds(0, 15)], es_sem)
    drained(blocks(7), gs1)
    drained(blocks(24), gs2)
    drained(blocks(32), gs3)
    drained(pieces(15), hs1)
    drained(blocks(24), hs2)
    drained(blocks(32), hs3)
    for n in range(2):
        drained(blocks(32), cs.at[n])
        drained(blocks(24), as_.at[n])
        drained(pieces(15), bs.at[n])
    landed(pieces(7), lr)
    for yy in range(4):
        block = jnp.concatenate([last[yy], last[4 + yy]], axis=0)
        out_ref[1, :, yy * 128:(yy + 1) * 128] = block.T
    drained(pieces(7), ls)


def per_device(ensemble, increment, obs_weight, vertical, block_table, block_cols):
    dma = pltpu.SemaphoreType.DMA
    vmem = pl.BlockSpec(memory_space=pltpu.VMEM)
    hbm = pl.BlockSpec(memory_space=pltpu.HBM)
    twice = lambda shape, kind=BF: [pltpu.VMEM(shape, kind)] * 2
    both = pl.pallas_call(
        kernel,
        out_shape=jax.ShapeDtypeStruct((2, 128, 512), BF),
        in_specs=[hbm] * 6,
        out_specs=vmem,
        scratch_shapes=[
            pltpu.SMEM((12, 64), jnp.int32),
            pltpu.VMEM((16, 128, 512), BF),
            pltpu.VMEM((64, 128, 128), BF),
            pltpu.VMEM((64, 128, 128), BF),
            pltpu.VMEM((128, 12 * 128), BF),
            pltpu.VMEM((128, 128), BF),
            pltpu.VMEM((128, 128), F32),
            pltpu.VMEM((128, 128), F32),
        ] + twice((2, 4, 4, 2, 128, 128)) + twice((4, 8, 128, 128)) + twice((4, 8, 128, 128))
        + twice((4, 4, 2, 128, 128)) + twice((3, 4, 2, 128, 128)) + twice((4, 2, 128, 128))
        + twice((16, 64, 128))
        + [
            pltpu.VMEM((8, 64, 128), BF),
            dma((6,)), dma, dma((16,)),
            dma, dma, dma, dma, dma, dma, dma, dma((4,)), dma, dma((4, 4)), dma, dma((4,)),
            dma((2,)), dma((2, 4)), dma((2,)), dma((2, 4)), dma((2,)), dma((2,)), dma, dma,
        ],
        compiler_params=pltpu.CompilerParams(
            collective_id=0, has_side_effects=True, vmem_limit_bytes=48 * 1024 * 1024),
        name="covariance",
    )(*[pltpu.with_memory_space_constraint(v, pltpu.HBM) for v in (ensemble, increment, obs_weight, vertical, block_table, block_cols.T)])
    return both[0].astype(F32), both[1].astype(F32)


def solution(mesh):
    return jax.shard_map(
        per_device,
        mesh=mesh,
        in_specs=(P("mem", None, "pts"), P(None, "pts"), P(None, "pts"), P(), P(), P()),
        out_specs=(P(None, "pts"), P(None, "pts")),
        check_vma=False,
    )
```

```python
import jax
import jax.numpy as jnp
from jax import lax
from jax.experimental import pallas as pl
from jax.experimental.pallas import tpu as pltpu
from jax.sharding import PartitionSpec as P

MESH = pl.DeviceIdType.MESH
BF = jnp.bfloat16
F32 = jnp.float32

SPREAD = (
    (0, 3, 0), (0, 1, 0), (1, 1, 1), (0, 3, 1), (1, 2, 1), (1, 3, 0), (1, 0, 0), (1, 0, 1),
    (0, 2, 1), (1, 2, 0), (1, 3, 1), (0, 1, 1), (0, 2, 0), (1, 1, 0), (0, 0, 1),
)
ORDER = (2, 1, 3, 0)
BACK = (2, 3, 1, 0)


def device(zhi, x, core, zlo, y):
    return ((zhi * 4 + x) * 2 + core, zlo * 4 + y)


def remote(src, dst, send, recv, to):
    return pltpu.make_async_remote_copy(
        src_ref=src, dst_ref=dst, send_sem=send, recv_sem=recv, device_id=to, device_id_type=MESH)


def kernel(
    ens_hbm, inc_hbm, obs_hbm, vert_hbm, table_hbm, cols_hbm,
    out_ref,
    cols_ref, arrived, ens, vl, tcat, vert, inc, obs,
    f1, f2, xo1, xo2, xi1, xi2, r1, r2, q1, q2, s1, s2, w1, w2, last,
    local_sem, es_sem, er_sem,
    gs1, gr1, gs2, gr2, gs3, gr3, hs1, hr1, hs2, hr2, hs3, hr3,
    cs, cr, as_, ar, bs, br, ls, lr,
):
    p, g = lax.axis_index("pts"), lax.axis_index("mem")
    zhi, x, core = p // 8, (p // 2) % 4, p % 2
    zlo, y = g // 4, g % 4
    zz = zhi * 2 + zlo
    other = 1 - core
    partner = device(zhi, x, other, zlo, y)
    flat = other
    a, b = flat * y + core * x, flat * x + core * y
    half = pl.ds(pl.multiple_of(zlo * 64, 64), 64)

    def ring_peer(a2):
        return device(zhi, flat * x + core * a2, core, zlo, flat * a2 + core * y)

    def plane_peer(b2, z2):
        return device(z2 // 2, flat * b2 + core * x, core, z2 % 2, flat * y + core * b2)

    def landed(ref, sem):
        remote(ref, ref, es_sem, sem, partner).wait_recv()

    def drained(ref, sem):
        remote(ref, ref, sem, er_sem.at[0], partner).wait_send()

    def blocks(n):
        return ens.at[pl.ds(0, n)]

    def pieces(n):
        return w1.at[pl.ds(0, n)]

    def block_of(core2, a2, b2, zh):
        return ((zh * 4 + (1 - core2) * b2 + core2 * a2) * 2 + core2) * 4 + (1 - core2) * a2 + core2 * b2

    mine = pl.ds(pl.multiple_of(y * 128, 128), 128)
    local = [
        pltpu.make_async_copy(inc_hbm.at[:, mine], inc, local_sem.at[0]),
        pltpu.make_async_copy(obs_hbm.at[:, mine], obs, local_sem.at[1]),
        pltpu.make_async_copy(ens_hbm.at[p], arrived.at[p], local_sem.at[2]),
        pltpu.make_async_copy(vert_hbm, vert, local_sem.at[3]),
    ]
    for s in range(12):
        local.append(pltpu.make_async_copy(
            table_hbm.at[s], tcat.at[:, pl.ds(s * 128, 128)], local_sem.at[4]))
    local.append(pltpu.make_async_copy(cols_hbm, cols_ref, local_sem.at[5]))
    for copy in local:
        copy.start()

    spread_to = [
        device((zhi + dz) % 2, (x + dx) % 4, (core + dc) % 2, zlo, y) for dz, dx, dc in SPREAD
    ]
    mem_peers = [(p, (g + d) % 8) for d in range(1, 8)]
    far = [
        device(flat * ((zhi + k // 4) % 2) + core * (1 - zhi), flat * ((x + k % 4) % 4) + core * x, core,
               flat * (1 - zlo) + core * ((zlo + k // 4) % 2), flat * y + core * ((y + k % 4) % 4))
        for k in range(1, 8)
    ]
    barrier = pltpu.get_barrier_semaphore()
    greet = spread_to + mem_peers + far
    for to in greet:
        pl.semaphore_signal(barrier, inc=1, device_id=to, device_id_type=MESH)

    local[0].wait()
    f1[core, y, x, zhi] = inc[...].T.astype(BF)

    def share(k):
        own = f1.at[core, y, x, zhi]
        copy = remote(own, own, gs1, gr1,
                      device((zhi + k // 4) % 2, (x + k % 4) % 4, core, zlo, y))
        copy.start()

    def spread(k):
        to = spread_to[k]
        copy = remote(ens_hbm.at[to[0]], arrived.at[p], es_sem, er_sem.at[p], to)
        copy.start()

    pl.semaphore_wait(barrier, len(greet))
    for k in (1, 3, 4, 2, 5, 7, 6):
        share(k)
    for k in range(15):
        spread(k)
    landed(blocks(7), gr1)
    own = f1.at[core, y]
    for d in (1, 2, 3):
        remote(own, own, gs2, gr2, device(zhi, x, core, zlo, (y + d) % 4)).start()
    landed(blocks(24), gr2)
    own = f1.at[core]
    remote(own, own, gs3, gr3, partner).start()
    landed(blocks(32), gr3)

    def mix(product):
        return lax.dot_general(product.astype(BF), vert[...], (((1,), (1,)), ((), ())),
                               preferred_element_type=F32).astype(BF)

    local[1].wait()
    obs[...] = obs[...].T
    local[3].wait()
    for k in range(16):
        dz, dx, dc = (0, 0, 0) if k == 0 else SPREAD[k - 1]
        zh, x2, core2 = (zhi + dz) % 2, (x + 4 - dx) % 4, (core + dc) % 2
        p2 = (zh * 4 + x2) * 2 + core2
        if k == 0:
            local[2].wait()
        else:
            landed(arrived.at[p2], er_sem.at[p2])
        products = []
        for yy in range(4):
            share = arrived[p2, :, yy * 128:(yy + 1) * 128].T
            ens[p2 * 4 + yy] = share
            products.append((share.astype(F32) * f1[core2, yy, x2, zh].astype(F32)).astype(BF))
        mixed = mix(jnp.concatenate(products, axis=0))
        for yy in range(4):
            vl[p2 * 4 + yy] = mixed[yy * 128:(yy + 1) * 128]
    pltpu.make_async_copy(tcat, tcat, local_sem.at[4]).wait()
    local[-1].wait()

    def vertical(f, core2, a2):
        products = []
        blocks = []
        for b2 in range(4):
            for zh in range(2):
                r = block_of(core2, a2, b2, zh)
                blocks.append(r)
                products.append((ens[r].astype(F32) * f[core2, a2, b2, zh].astype(F32)).astype(BF))
        mixed = mix(jnp.concatenate(products, axis=0))
        for k, r in enumerate(blocks):
            vl[r] = mixed[k * 128:(k + 1) * 128]

    def horizontal(core2, a2):
        blocks = [block_of(core2, a2, b2, zh) for b2 in range(4) for zh in range(2)]
        stacked = jnp.concatenate(
            [jnp.concatenate([vl[cols_ref[s, r]] for s in range(12)], axis=0) for r in blocks], axis=1)
        total = jnp.dot(tcat[...], stacked, preferred_element_type=F32).astype(BF)
        return [ens[r].astype(F32) * total[:, k * 128:(k + 1) * 128].astype(F32)
                for k, r in enumerate(blocks)]

    def step_of(t):
        return jnp.where(t == 0, 2, jnp.where(t == 1, 1, jnp.where(t == 2, 3, 0)))

    def scatter(n, xo, xi, r, q, s_buf, w):
        a_other = flat * x + core * y

        def core_copy(t):
            return remote(xo.at[t], xi.at[t], cs.at[n], cr.at[n, t], partner)

        def away(t):
            for k, value in enumerate(horizontal(other, (a_other + step_of(t)) % 4)):
                xo[t, k] = value.astype(BF)
            core_copy(t).start()

        def keep(t):
            values = horizontal(core, (a + step_of(t)) % 4)
            core_copy(t).wait_recv()
            for k, value in enumerate(values):
                r[t, k // 2, k % 2] = (value + xi[t, k].astype(F32)).astype(BF)

        def ring_copy(t, b2):
            return remote(r.at[t, b2], q.at[t, b2], as_.at[n], ar.at[n, b2],
                          ring_peer((a + step_of(t)) % 4))

        def both(t, carry):
            away(t + 1)
            keep(t)
            for d in ORDER:
                ring_copy(t, (b + d) % 4).start()
            return carry

        away(0)
        lax.fori_loop(0, 3, both, 0)
        keep(3)

        def plane_copy(b2, z2):
            rows = pl.ds(pl.multiple_of((z2 % 2) * 64, 64), 64)
            return remote(s_buf.at[b2, z2 // 2, rows], w.at[b * 4 + zz], bs.at[n],
                          br.at[n], plane_peer(b2, z2))

        for d in ORDER:
            b2 = (b + d) % 4
            total = r[3, b2].astype(F32)
            landed(blocks(6), ar.at[n, b2])
            for t in range(3):
                total = total + q[t, b2].astype(F32)
            s_buf[b2] = total.astype(BF)
            for dz in ORDER:
                if d or dz:
                    plane_copy(b2, (zz + dz) % 4).start()
        total = s_buf[b, zhi, half].astype(F32)
        landed(pieces(15), br.at[n])
        for d in BACK:
            for dz in BACK:
                if d or dz:
                    k = (b + d) % 4 * 4 + (zz + dz) % 4
                    total = total + w[k].astype(F32)

        return total

    first = scatter(0, xo1, xi1, r1, q1, s1, w1)

    f2[core, a, b, zhi, half] = (first * obs[half]).astype(BF)

    def piece(d, dz):
        b2, z2 = (b + d) % 4, (zz + dz) % 4
        rows = pl.ds(pl.multiple_of((z2 % 2) * 64, 64), 64)
        return f2.at[core, a, b2, z2 // 2, rows], b2

    def pass_on(d, dz):
        slot, b2 = piece(d, dz)
        for da in (1, 3, 2):
            remote(slot, slot, hs2, hr2.at[a, b2], ring_peer((a + da) % 4)).start()

    pass_on(0, 0)
    own, b2 = piece(0, 0)
    for d in (0, 1, 3, 2):
        for dz in (2, 1, 3, 0):
            if d or dz:
                remote(own, own, hs1, hr1.at[b * 4 + zz], plane_peer((b + d) % 4, (zz + dz) % 4)).start()
    for d in (0, 3, 1, 2):
        for dz in (0, 1, 3, 2):
            if d or dz:
                landed(pieces(1), hr1.at[(b + d) % 4 * 4 + (zz + dz) % 4])
                pass_on(d, dz)

    def hand_over(a2):
        slot = f2.at[core, a2]
        remote(slot, slot, hs3, hr3.at[a2], partner).start()

    def take(da):
        a2 = (flat * x + core * y + da) % 4
        landed(blocks(8), hr3.at[a2])
        vertical(f2, other, a2)

    hand_over(a)
    vertical(f2, core, a)
    before = 0
    for da in (1, 3, 2):
        a2 = (a + da) % 4
        for d in (0, 3, 1, 2):
            b2 = (b + d) % 4
            landed(blocks(2), hr2.at[a2, b2])
            slot = f2.at[core, a2, b2]
            remote(slot, slot, hs3, hr3.at[a2], partner).start()
        vertical(f2, core, a2)
        take(before)
        before = da
    take(2)
    second = scatter(1, xo2, xi2, r2, q2, s2, w2)

    last[g] = second.astype(BF)
    for to in mem_peers:
        remote(last.at[g], last.at[g], ls, lr, to).start()
    for yy in range(4):
        block = f2[core, flat * yy + core * x, flat * x + core * yy, zhi]
        out_ref[0, :, yy * 128:(yy + 1) * 128] = block.T
    drained(arrived.at[pl.ds(0, 15)], es_sem)
    drained(blocks(7), gs1)
    drained(blocks(24), gs2)
    drained(blocks(32), gs3)
    drained(pieces(15), hs1)
    drained(blocks(24), hs2)
    drained(blocks(32), hs3)
    for n in range(2):
        drained(blocks(32), cs.at[n])
        drained(blocks(24), as_.at[n])
        drained(pieces(15), bs.at[n])
    landed(pieces(7), lr)
    for yy in range(4):
        block = jnp.concatenate([last[yy], last[4 + yy]], axis=0)
        out_ref[1, :, yy * 128:(yy + 1) * 128] = block.T
    drained(pieces(7), ls)


def per_device(ensemble, increment, obs_weight, vertical, block_table, block_cols):
    dma = pltpu.SemaphoreType.DMA
    vmem = pl.BlockSpec(memory_space=pltpu.VMEM)
    hbm = pl.BlockSpec(memory_space=pltpu.HBM)
    twice = lambda shape, kind=BF: [pltpu.VMEM(shape, kind)] * 2
    both = pl.pallas_call(
        kernel,
        out_shape=jax.ShapeDtypeStruct((2, 128, 512), BF),
        in_specs=[hbm] * 6,
        out_specs=vmem,
        scratch_shapes=[
            pltpu.SMEM((12, 64), jnp.int32),
            pltpu.VMEM((16, 128, 512), BF),
            pltpu.VMEM((64, 128, 128), BF),
            pltpu.VMEM((64, 128, 128), BF),
            pltpu.VMEM((128, 12 * 128), BF),
            pltpu.VMEM((128, 128), BF),
            pltpu.VMEM((128, 128), F32),
            pltpu.VMEM((128, 128), F32),
        ] + twice((2, 4, 4, 2, 128, 128)) + twice((4, 8, 128, 128)) + twice((4, 8, 128, 128))
        + twice((4, 4, 2, 128, 128)) + twice((3, 4, 2, 128, 128)) + twice((4, 2, 128, 128))
        + twice((16, 64, 128))
        + [
            pltpu.VMEM((8, 64, 128), BF),
            dma((6,)), dma, dma((16,)),
            dma, dma, dma, dma, dma, dma, dma, dma((16,)), dma, dma((4, 4)), dma, dma((4,)),
            dma((2,)), dma((2, 4)), dma((2,)), dma((2, 4)), dma((2,)), dma((2,)), dma, dma,
        ],
        compiler_params=pltpu.CompilerParams(
            collective_id=0, has_side_effects=True, vmem_limit_bytes=48 * 1024 * 1024),
        name="covariance",
    )(*[pltpu.with_memory_space_constraint(v, pltpu.HBM) for v in (ensemble, increment, obs_weight, vertical, block_table, block_cols.T)])
    return both[0].astype(F32), both[1].astype(F32)


def solution(mesh):
    return jax.shard_map(
        per_device,
        mesh=mesh,
        in_specs=(P("mem", None, "pts"), P(None, "pts"), P(None, "pts"), P(), P(), P()),
        out_specs=(P(None, "pts"), P(None, "pts")),
        check_vma=False,
    )
```

```python
import jax
import jax.numpy as jnp
from jax import lax
from jax.experimental import pallas as pl
from jax.experimental.pallas import tpu as pltpu
from jax.sharding import PartitionSpec as P

MESH = pl.DeviceIdType.MESH
BF = jnp.bfloat16
F32 = jnp.float32

SPREAD = (
    (0, 3, 0), (0, 1, 0), (1, 1, 1), (0, 3, 1), (1, 2, 1), (1, 3, 0), (1, 0, 0), (1, 0, 1),
    (0, 2, 1), (1, 2, 0), (1, 3, 1), (0, 1, 1), (0, 2, 0), (1, 1, 0), (0, 0, 1),
)
ORDER = (2, 1, 3, 0)
BACK = (2, 3, 1, 0)


def device(zhi, x, core, zlo, y):
    return ((zhi * 4 + x) * 2 + core, zlo * 4 + y)


def remote(src, dst, send, recv, to):
    return pltpu.make_async_remote_copy(
        src_ref=src, dst_ref=dst, send_sem=send, recv_sem=recv, device_id=to, device_id_type=MESH)


def kernel(
    ens_hbm, inc_hbm, obs_hbm, vert_hbm, table_hbm, cols_hbm,
    out_ref,
    cols_ref, arrived, ens, vl, tcat, vert, inc, obs,
    f1, f2, xo1, xo2, xi1, xi2, r1, r2, q1, q2, s1, s2, w1, w2, last,
    local_sem, es_sem, er_sem,
    gs1, gr1, gs2, gr2, gs3, gr3, hs1, hr1, hs2, hr2, hs3, hr3,
    cs, cr, as_, ar, bs, br, ls, lr,
):
    p, g = lax.axis_index("pts"), lax.axis_index("mem")
    zhi, x, core = p // 8, (p // 2) % 4, p % 2
    zlo, y = g // 4, g % 4
    zz = zhi * 2 + zlo
    other = 1 - core
    partner = device(zhi, x, other, zlo, y)
    flat = other
    a, b = flat * y + core * x, flat * x + core * y
    half = pl.ds(pl.multiple_of(zlo * 64, 64), 64)

    def ring_peer(a2):
        return device(zhi, flat * x + core * a2, core, zlo, flat * a2 + core * y)

    def plane_peer(b2, z2):
        return device(z2 // 2, flat * b2 + core * x, core, z2 % 2, flat * y + core * b2)

    def landed(ref, sem):
        remote(ref, ref, es_sem, sem, partner).wait_recv()

    def drained(ref, sem):
        remote(ref, ref, sem, er_sem.at[0], partner).wait_send()

    def blocks(n):
        return ens.at[pl.ds(0, n)]

    def pieces(n):
        return w1.at[pl.ds(0, n)]

    def block_of(core2, a2, b2, zh):
        return ((zh * 4 + (1 - core2) * b2 + core2 * a2) * 2 + core2) * 4 + (1 - core2) * a2 + core2 * b2

    mine = pl.ds(pl.multiple_of(y * 128, 128), 128)
    local = [
        pltpu.make_async_copy(inc_hbm.at[:, mine], inc, local_sem.at[0]),
        pltpu.make_async_copy(obs_hbm.at[:, mine], obs, local_sem.at[1]),
        pltpu.make_async_copy(ens_hbm.at[p], arrived.at[p], local_sem.at[2]),
        pltpu.make_async_copy(vert_hbm, vert, local_sem.at[3]),
    ]
    for s in range(12):
        local.append(pltpu.make_async_copy(
            table_hbm.at[s], tcat.at[:, pl.ds(s * 128, 128)], local_sem.at[4]))
    local.append(pltpu.make_async_copy(cols_hbm, cols_ref, local_sem.at[5]))
    for copy in local:
        copy.start()

    spread_to = [
        device((zhi + dz) % 2, (x + dx) % 4, (core + dc) % 2, zlo, y) for dz, dx, dc in SPREAD
    ]
    mem_peers = [(p, (zlo + dz) % 2 * 4 + (y + dy) % 4)
                 for dz, dy in ((1, 2), (1, 1), (1, 3), (0, 2), (0, 1), (0, 3), (1, 0))]
    far = [
        device(flat * ((zhi + k // 4) % 2) + core * (1 - zhi), flat * ((x + k % 4) % 4) + core * x, core,
               flat * (1 - zlo) + core * ((zlo + k // 4) % 2), flat * y + core * ((y + k % 4) % 4))
        for k in range(1, 8)
    ]
    barrier = pltpu.get_barrier_semaphore()
    greet = spread_to + mem_peers + far
    for to in greet:
        pl.semaphore_signal(barrier, inc=1, device_id=to, device_id_type=MESH)

    local[0].wait()
    f1[core, y, x, zhi] = inc[...].T.astype(BF)

    def share(k):
        own = f1.at[core, y, x, zhi]
        copy = remote(own, own, gs1, gr1,
                      device((zhi + k // 4) % 2, (x + k % 4) % 4, core, zlo, y))
        copy.start()

    def spread(k):
        to = spread_to[k]
        copy = remote(ens_hbm.at[to[0]], arrived.at[p], es_sem, er_sem.at[p], to)
        copy.start()

    pl.semaphore_wait(barrier, len(greet))
    for k in (1, 3, 4, 2, 5, 7, 6):
        share(k)
    for k in range(15):
        spread(k)
    landed(blocks(7), gr1)
    own = f1.at[core, y]
    for d in (1, 2, 3):
        remote(own, own, gs2, gr2, device(zhi, x, core, zlo, (y + d) % 4)).start()
    landed(blocks(24), gr2)
    own = f1.at[core]
    remote(own, own, gs3, gr3, partner).start()
    landed(blocks(32), gr3)

    def mix(product):
        return lax.dot_general(product.astype(BF), vert[...], (((1,), (1,)), ((), ())),
                               preferred_element_type=F32).astype(BF)

    local[1].wait()
    obs[...] = obs[...].T
    local[3].wait()
    for k in range(16):
        dz, dx, dc = (0, 0, 0) if k == 0 else SPREAD[k - 1]
        zh, x2, core2 = (zhi + dz) % 2, (x + 4 - dx) % 4, (core + dc) % 2
        p2 = (zh * 4 + x2) * 2 + core2
        if k == 0:
            local[2].wait()
        else:
            landed(arrived.at[p2], er_sem.at[p2])
        products = []
        for yy in range(4):
            share = arrived[p2, :, yy * 128:(yy + 1) * 128].T
            ens[p2 * 4 + yy] = share
            products.append((share.astype(F32) * f1[core2, yy, x2, zh].astype(F32)).astype(BF))
        mixed = mix(jnp.concatenate(products, axis=0))
        for yy in range(4):
            vl[p2 * 4 + yy] = mixed[yy * 128:(yy + 1) * 128]
    pltpu.make_async_copy(tcat, tcat, local_sem.at[4]).wait()
    local[-1].wait()

    def vertical(f, core2, a2):
        products = []
        blocks = []
        for b2 in range(4):
            for zh in range(2):
                r = block_of(core2, a2, b2, zh)
                blocks.append(r)
                products.append((ens[r].astype(F32) * f[core2, a2, b2, zh].astype(F32)).astype(BF))
        mixed = mix(jnp.concatenate(products, axis=0))
        for k, r in enumerate(blocks):
            vl[r] = mixed[k * 128:(k + 1) * 128]

    def horizontal(core2, a2):
        blocks = [block_of(core2, a2, b2, zh) for b2 in range(4) for zh in range(2)]
        stacked = jnp.concatenate(
            [jnp.concatenate([vl[cols_ref[s, r]] for s in range(12)], axis=0) for r in blocks], axis=1)
        total = jnp.dot(tcat[...], stacked, preferred_element_type=F32).astype(BF)
        return [ens[r].astype(F32) * total[:, k * 128:(k + 1) * 128].astype(F32)
                for k, r in enumerate(blocks)]

    def step_of(t):
        return jnp.where(t == 0, 2, jnp.where(t == 1, 1, jnp.where(t == 2, 3, 0)))

    def scatter(n, xo, xi, r, q, s_buf, w):
        a_other = flat * x + core * y

        def core_copy(t):
            return remote(xo.at[t], xi.at[t], cs.at[n], cr.at[n, t], partner)

        def away(t):
            for k, value in enumerate(horizontal(other, (a_other + step_of(t)) % 4)):
                xo[t, k] = value.astype(BF)
            core_copy(t).start()

        def keep(t):
            values = horizontal(core, (a + step_of(t)) % 4)
            core_copy(t).wait_recv()
            for k, value in enumerate(values):
                r[t, k // 2, k % 2] = (value + xi[t, k].astype(F32)).astype(BF)

        def ring_copy(t, b2):
            return remote(r.at[t, b2], q.at[t, b2], as_.at[n], ar.at[n, b2],
                          ring_peer((a + step_of(t)) % 4))

        def both(t, carry):
            away(t + 1)
            keep(t)
            for d in ORDER:
                ring_copy(t, (b + d) % 4).start()
            return carry

        away(0)
        lax.fori_loop(0, 3, both, 0)
        keep(3)

        def plane_copy(b2, z2):
            rows = pl.ds(pl.multiple_of((z2 % 2) * 64, 64), 64)
            return remote(s_buf.at[b2, z2 // 2, rows], w.at[b * 4 + zz], bs.at[n],
                          br.at[n], plane_peer(b2, z2))

        for d in ORDER:
            b2 = (b + d) % 4
            total = r[3, b2].astype(F32)
            landed(blocks(6), ar.at[n, b2])
            for t in range(3):
                total = total + q[t, b2].astype(F32)
            s_buf[b2] = total.astype(BF)
            for dz in ORDER:
                if d or dz:
                    plane_copy(b2, (zz + dz) % 4).start()
        total = s_buf[b, zhi, half].astype(F32)
        landed(pieces(15), br.at[n])
        for d in BACK:
            for dz in BACK:
                if d or dz:
                    k = (b + d) % 4 * 4 + (zz + dz) % 4
                    total = total + w[k].astype(F32)

        return total

    first = scatter(0, xo1, xi1, r1, q1, s1, w1)

    f2[core, a, b, zhi, half] = (first * obs[half]).astype(BF)

    def piece(d, dz):
        b2, z2 = (b + d) % 4, (zz + dz) % 4
        rows = pl.ds(pl.multiple_of((z2 % 2) * 64, 64), 64)
        return f2.at[core, a, b2, z2 // 2, rows], b2

    def pass_on(d, dz):
        slot, b2 = piece(d, dz)
        for da in (1, 3, 2):
            remote(slot, slot, hs2, hr2.at[a, b2], ring_peer((a + da) % 4)).start()

    pass_on(0, 0)
    own, b2 = piece(0, 0)
    for d in (0, 1, 3, 2):
        for dz in (2, 1, 3, 0):
            if d or dz:
                remote(own, own, hs1, hr1.at[b * 4 + zz], plane_peer((b + d) % 4, (zz + dz) % 4)).start()
    for d in (0, 3, 1, 2):
        for dz in (0, 1, 3, 2):
            if d or dz:
                landed(pieces(1), hr1.at[(b + d) % 4 * 4 + (zz + dz) % 4])
                pass_on(d, dz)

    def hand_over(a2):
        slot = f2.at[core, a2]
        remote(slot, slot, hs3, hr3.at[a2], partner).start()

    def take(da):
        a2 = (flat * x + core * y + da) % 4
        landed(blocks(8), hr3.at[a2])
        vertical(f2, other, a2)

    hand_over(a)
    vertical(f2, core, a)
    before = 0
    for da in (1, 3, 2):
        a2 = (a + da) % 4
        for d in (0, 3, 1, 2):
            b2 = (b + d) % 4
            landed(blocks(2), hr2.at[a2, b2])
            slot = f2.at[core, a2, b2]
            remote(slot, slot, hs3, hr3.at[a2], partner).start()
        vertical(f2, core, a2)
        take(before)
        before = da
    take(2)
    second = scatter(1, xo2, xi2, r2, q2, s2, w2)

    last[g] = second.astype(BF)
    for to in mem_peers:
        remote(last.at[g], last.at[g], ls, lr, to).start()
    for yy in range(4):
        block = f2[core, flat * yy + core * x, flat * x + core * yy, zhi]
        out_ref[0, :, yy * 128:(yy + 1) * 128] = block.T
    drained(arrived.at[pl.ds(0, 15)], es_sem)
    drained(blocks(7), gs1)
    drained(blocks(24), gs2)
    drained(blocks(32), gs3)
    drained(pieces(15), hs1)
    drained(blocks(24), hs2)
    drained(blocks(32), hs3)
    for n in range(2):
        drained(blocks(32), cs.at[n])
        drained(blocks(24), as_.at[n])
        drained(pieces(15), bs.at[n])
    landed(pieces(7), lr)
    for yy in range(4):
        block = jnp.concatenate([last[yy], last[4 + yy]], axis=0)
        out_ref[1, :, yy * 128:(yy + 1) * 128] = block.T
    drained(pieces(7), ls)


def per_device(ensemble, increment, obs_weight, vertical, block_table, block_cols):
    dma = pltpu.SemaphoreType.DMA
    vmem = pl.BlockSpec(memory_space=pltpu.VMEM)
    hbm = pl.BlockSpec(memory_space=pltpu.HBM)
    twice = lambda shape, kind=BF: [pltpu.VMEM(shape, kind)] * 2
    both = pl.pallas_call(
        kernel,
        out_shape=jax.ShapeDtypeStruct((2, 128, 512), BF),
        in_specs=[hbm] * 6,
        out_specs=vmem,
        scratch_shapes=[
            pltpu.SMEM((12, 64), jnp.int32),
            pltpu.VMEM((16, 128, 512), BF),
            pltpu.VMEM((64, 128, 128), BF),
            pltpu.VMEM((64, 128, 128), BF),
            pltpu.VMEM((128, 12 * 128), BF),
            pltpu.VMEM((128, 128), BF),
            pltpu.VMEM((128, 128), F32),
            pltpu.VMEM((128, 128), F32),
        ] + twice((2, 4, 4, 2, 128, 128)) + twice((4, 8, 128, 128)) + twice((4, 8, 128, 128))
        + twice((4, 4, 2, 128, 128)) + twice((3, 4, 2, 128, 128)) + twice((4, 2, 128, 128))
        + twice((16, 64, 128))
        + [
            pltpu.VMEM((8, 64, 128), BF),
            dma((6,)), dma, dma((16,)),
            dma, dma, dma, dma, dma, dma, dma, dma((16,)), dma, dma((4, 4)), dma, dma((4,)),
            dma((2,)), dma((2, 4)), dma((2,)), dma((2, 4)), dma((2,)), dma((2,)), dma, dma,
        ],
        compiler_params=pltpu.CompilerParams(
            collective_id=0, has_side_effects=True, vmem_limit_bytes=48 * 1024 * 1024),
        name="covariance",
    )(*[pltpu.with_memory_space_constraint(v, pltpu.HBM) for v in (ensemble, increment, obs_weight, vertical, block_table, block_cols.T)])
    return both[0].astype(F32), both[1].astype(F32)


def solution(mesh):
    return jax.shard_map(
        per_device,
        mesh=mesh,
        in_specs=(P("mem", None, "pts"), P(None, "pts"), P(None, "pts"), P(), P(), P()),
        out_specs=(P(None, "pts"), P(None, "pts")),
        check_vma=False,
    )
```
